32 devices in a mesh: ctx: 8 (over y, x, core), ch: 4 (over z).
Axes of the slice: x: 2, y: 2, z: 4, core: 2. Of those that a mesh axis runs over, the one named last changes fastest.
Arguments:
- inputs: bfloat16 [1024, 1536], P('ctx', 'ch'), may hold values from -6 to 6
- grad_out: bfloat16 [1024, 1536], P('ctx', 'ch'), may hold values from -6 to 6
- filter_w: bfloat16 [12, 1024], P('ch', 'ctx'), may hold values from -6 to 6
Outputs:
- input_grad: bfloat16 [1024, 1536], P('ctx', 'ch')
- filter_grad: float32 [12, 1024], P('ch', 'ctx')
The draws below stay inside these ranges and needn't reach their ends.
All inputs are finite; a program needn't handle non-finite values.
Results may differ from the reference program's by a relative error of at most 0.001.
Values may be sent and summed in bfloat16 or wider, within the bound.
No kernel may reach another device: no remote copies, remote signals or barrier semaphores. Data moves between devices by JAX's collectives and lax.ppermute only.
A program may use at most 64 MiB of HBM per device.

```python
import jax
import jax.numpy as jnp
from jax import lax

HEAD_W = 128
TOK_DEV = 128
HEADS = 12
CHANNELS = 1536
TOKENS = 1024
N_CTX = 8


def steps_of(stream_key, dims, cuts, smallest, largest):
    loudness = 1.0
    for dim, shards_of in cuts:
        draws = jax.random.uniform(jax.random.fold_in(jax.random.fold_in(stream_key, 6), dim), (shards_of,), jnp.float32, smallest / len(cuts), largest / len(cuts))
        loudness = loudness * jnp.repeat(jnp.exp(draws), dims[dim] // shards_of).reshape((-1,) + (1,) * (len(dims) - 1 - dim))
    return loudness


def scatter_about(stream_key, shape, deviation, bound, pieces=(), kind=jnp.bfloat16):
    drawn = jax.random.normal(stream_key, shape, jnp.float32) * deviation
    if len(pieces) > 0:
        drawn = steps_of(stream_key, shape, pieces, -0.22, 0.18) * drawn
    return jnp.clip(drawn, min=-bound, max=bound).astype(kind)


def setup_inputs(seed: int = 0) -> dict:
    arg_keys = jax.random.split(jax.random.key(seed), 4)
    return {
        "inputs": scatter_about(arg_keys[0], (TOKENS, CHANNELS), 1.0, 6.0, ((0, 8), (1, 4))),
        "grad_out": scatter_about(arg_keys[1], (TOKENS, CHANNELS), 1.0, 6.0, ((0, 8), (1, 4))),
        "filter_w": scatter_about(arg_keys[2], (HEADS, TOKENS), 1.0, 6.0, ((0, 4), (1, 8))),
    }


def toeplitz_of(window, rows):
    heads = window.shape[0]
    reversed_window = window[:, ::-1]
    repeated = jnp.broadcast_to(reversed_window[:, None, :], (heads, rows, 2 * rows)).reshape(heads, 2 * rows * rows)
    skewed = repeated[:, :rows * (2 * rows - 1)].reshape(heads, rows, 2 * rows - 1)
    return skewed[:, :, rows - 1:2 * rows - 1]


def diagonal_terms(products, rows):
    heads = products.shape[0]
    flipped = products[:, :, ::-1]
    padded = jnp.pad(flipped, ((0, 0), (0, 0), (0, rows + 1)))
    sheared = padded.reshape(heads, rows * (2 * rows + 1))[:, :2 * rows * rows].reshape(heads, rows, 2 * rows)
    diagonal_sums = jnp.sum(sheared, axis=1)
    return jnp.concatenate([jnp.zeros((heads, 1), diagonal_sums.dtype), diagonal_sums[:, :2 * rows - 1]], axis=1)


def reference(inputs, grad_out, filter_w):
    rows = TOK_DEV
    blocks = N_CTX
    heads = HEADS
    input_blocks = inputs.astype(jnp.float32).reshape(blocks, rows, heads, HEAD_W)
    grad_blocks = grad_out.astype(jnp.float32).reshape(blocks, rows, heads, HEAD_W)
    padded_filter = jnp.concatenate([jnp.zeros((heads, rows), jnp.float32), filter_w.astype(jnp.float32)], axis=1)
    block_ids = jnp.arange(blocks, dtype=jnp.int32)

    def advance(state_now, lag_index):
        input_acc, padded_grad = state_now
        lag_start = (lag_index * rows).astype(jnp.int32)
        window = lax.dynamic_slice_in_dim(padded_filter, lag_start, 2 * rows, 1)
        toeplitz = toeplitz_of(window, rows)
        live = (block_ids + lag_index < blocks).astype(jnp.float32)[:, None, None, None]
        shifted = jnp.roll(grad_blocks, -lag_index, axis=0) * live
        contribution = jnp.einsum("gts,itgc->isgc", toeplitz, shifted, precision=lax.Precision.HIGHEST)
        input_acc = input_acc + contribution
        products = jnp.einsum("itgc,isgc->gts", shifted, input_blocks, precision=lax.Precision.HIGHEST)
        window_grad = diagonal_terms(products, rows)
        current = lax.dynamic_slice_in_dim(padded_grad, lag_start, 2 * rows, 1)
        padded_grad = lax.dynamic_update_slice_in_dim(padded_grad, current + window_grad, lag_start, 1)
        return (input_acc, padded_grad), None

    start_state = (jnp.zeros((blocks, rows, heads, HEAD_W), jnp.float32), jnp.zeros((heads, TOKENS + rows), jnp.float32))
    (input_acc, padded_grad), _ = lax.scan(advance, start_state, block_ids)
    factor = float(TOKENS) ** -0.5
    input_grad = (input_acc.reshape(TOKENS, CHANNELS) * factor).astype(jnp.bfloat16)
    filter_grad = padded_grad[:, rows:] * factor
    return input_grad, filter_grad
```

```python
import functools

import jax
import jax.numpy as jnp
from jax import lax
from jax.experimental import pallas as pl
from jax.experimental.pallas import tpu as pltpu
from jax.sharding import PartitionSpec as P

EXTRA = 8
VMEM = pltpu.VMEM


def pack_kernel(grad_ref, input_ref, filter_ref, out_ref, filter_vmem, sems):
    rows = grad_ref.shape[0]
    heads = filter_ref.shape[0]
    width = filter_ref.shape[1]
    copies = [
        pltpu.make_async_copy(filter_ref, filter_vmem, sems.at[0]),
        pltpu.make_async_copy(grad_ref, out_ref.at[pl.ds(0, rows)], sems.at[1]),
        pltpu.make_async_copy(input_ref, out_ref.at[pl.ds(rows, rows)], sems.at[2]),
    ]
    for copy in copies:
        copy.start()
    copies[0].wait()
    block = filter_vmem[...].astype(jnp.float32)
    block = jnp.concatenate([block, jnp.zeros((EXTRA - heads, width), jnp.float32)], axis=0)
    out_ref[2 * rows :, :width] = block.astype(out_ref.dtype)
    out_ref[2 * rows :, width:] = jnp.zeros((EXTRA, out_ref.shape[1] - width), out_ref.dtype)
    copies[1].wait()
    copies[2].wait()


def repeat(count, step, start):
    if count <= 4:
        for index in range(count):
            start = step(index, start)
        return start
    return lax.fori_loop(0, count, step, start)


def main_kernel(heads, factor, mine_ref, theirs_ref, out_ref, terms_ref, lags_ref, toeplitz_ref, out_vmem, terms_vmem, sems):
    half, span, channels = mine_ref.shape
    rows = (span - EXTRA) // 2
    width = channels // heads
    blocks = 2 * half
    position = lax.axis_index("ctx")
    pair = position // 2
    core = position - 2 * pair

    lags_ref[...] = jnp.zeros_like(lags_ref)

    def place(slot, carry):
        for ref, parity in ((mine_ref, core), (theirs_ref, 1 - core)):
            at = pl.multiple_of((blocks + 1 + 2 * slot + parity) * rows, rows)
            lags_ref[:, pl.ds(at, rows)] = ref[slot, 2 * rows :, :rows].astype(jnp.float32)
        return carry

    repeat(half, place, 0)
    start = pl.multiple_of((blocks - position) * rows, rows)
    window = lags_ref[:, pl.ds(start, (blocks + 1) * rows)]
    reach = (blocks + 1) * rows
    for head in range(heads):
        lines = jnp.broadcast_to(window[head : head + 1], (rows, reach))
        skewed = pltpu.roll(lines, 0, 1, stride=1, stride_axis=0)
        toeplitz_ref[head] = skewed[:, rows:].astype(toeplitz_ref.dtype)

    def compute(even_ref, odd_ref, parity):
        for head in range(heads):
            lanes = slice(head * width, (head + 1) * width)

            def accumulate(slot, total):
                both = jnp.concatenate([even_ref[slot, :rows, lanes], odd_ref[slot, :rows, lanes]], axis=0)
                at = slot * 2 * rows if isinstance(slot, int) else pl.multiple_of(slot * 2 * rows, 2 * rows)
                return total + jnp.dot(
                    toeplitz_ref[head, :, pl.ds(at, 2 * rows)], both, preferred_element_type=jnp.float32
                )

            total = repeat(half, accumulate, jnp.zeros((rows, width), jnp.float32))
            out_vmem[:, lanes] = (total * factor).astype(out_vmem.dtype)
            pltpu.make_async_copy(out_vmem.at[:, lanes], out_ref.at[:, lanes], sems.at[head]).start()

        sums = []
        for head in range(heads):
            lanes = slice(head * width, (head + 1) * width)

            def grad_at(ref, slot):
                held = ref[jnp.minimum(slot, half - 1), :rows, lanes]
                return jnp.where(slot < half, held, jnp.zeros_like(held))

            def accumulate(slot, total):
                mid = slot + pair
                if parity == 0:
                    first, second, third = grad_at(even_ref, mid), grad_at(odd_ref, mid), grad_at(even_ref, mid + 1)
                else:
                    first, second, third = grad_at(odd_ref, mid), grad_at(even_ref, mid + 1), grad_at(odd_ref, mid + 1)
                left = jnp.concatenate(
                    [even_ref[slot, rows : 2 * rows, lanes], odd_ref[slot, rows : 2 * rows, lanes]], axis=1
                )
                right = jnp.concatenate(
                    [jnp.concatenate([first, second], axis=1), jnp.concatenate([second, third], axis=1)], axis=0
                )
                return total + lax.dot_general(
                    left, right, (((1,), (1,)), ((), ())), preferred_element_type=jnp.float32
                )

            products = repeat(half, accumulate, jnp.zeros((rows, 2 * rows), jnp.float32))
            folded = products[0:8]
            for group in range(1, rows // 8):
                folded = folded + pltpu.roll(products[8 * group : 8 * group + 8], 2 * rows - 8 * group, 1)
            sums.append(folded)
        folded = jnp.concatenate(sums, axis=0)
        line = lax.broadcasted_iota(jnp.int32, folded.shape, 0)
        for bit in (1, 2, 4):
            folded = jnp.where((line & bit) != 0, pltpu.roll(folded, 2 * rows - bit, 1), folded)
        for head in range(heads):
            terms_vmem[head : head + 1, :] = (
                jnp.sum(folded[8 * head : 8 * head + 8, :rows], axis=0, keepdims=True) * factor
            )

    @pl.when(core == 0)
    def _():
        compute(mine_ref, theirs_ref, 0)

    @pl.when(core == 1)
    def _():
        compute(theirs_ref, mine_ref, 1)

    last = pltpu.make_async_copy(terms_vmem, terms_ref, sems.at[heads])
    last.start()
    for head in range(heads):
        lanes = slice(head * width, (head + 1) * width)
        pltpu.make_async_copy(out_vmem.at[:, lanes], out_ref.at[:, lanes], sems.at[head]).wait()
    last.wait()


def body(inputs, grad_out, filter_w):
    rows, channels = inputs.shape
    heads = filter_w.shape[0]
    blocks = lax.axis_size("ctx")
    half = blocks // 2
    factor = float(rows * blocks) ** (-0.5)
    anywhere = pl.BlockSpec(memory_space=pl.ANY)
    on_chip = pl.BlockSpec(memory_space=VMEM)
    span = 2 * rows + EXTRA
    payload = pl.pallas_call(
        pack_kernel,
        out_shape=jax.ShapeDtypeStruct((span, channels), inputs.dtype),
        in_specs=[anywhere] * 3,
        out_specs=on_chip,
        scratch_shapes=[VMEM(filter_w.shape, filter_w.dtype), pltpu.SemaphoreType.DMA((3,))],
        name="pack",
    )(grad_out, inputs, filter_w)
    groups = [[2 * slot + core for slot in range(half)] for core in range(2)]
    mine = lax.all_gather(payload, "ctx", axis=0, tiled=False, axis_index_groups=groups)
    theirs = lax.ppermute(mine, "ctx", [(index, index ^ 1) for index in range(blocks)])
    return pl.pallas_call(
        functools.partial(main_kernel, heads, factor),
        out_shape=(
            jax.ShapeDtypeStruct((rows, channels), inputs.dtype),
            jax.ShapeDtypeStruct((heads, rows), jnp.float32),
        ),
        in_specs=[on_chip] * 2,
        out_specs=(anywhere, anywhere),
        scratch_shapes=[
            VMEM((EXTRA, (2 * blocks + 1) * rows), jnp.float32),
            VMEM((heads, rows, blocks * rows), inputs.dtype),
            VMEM((rows, channels), inputs.dtype),
            VMEM((heads, rows), jnp.float32),
            pltpu.SemaphoreType.DMA((heads + 1,)),
        ],
        name="main",
    )(mine, theirs)


def solution(mesh):
    placed = (P("ctx", "ch"), P("ctx", "ch"), P("ch", "ctx"))
    return jax.shard_map(
        body,
        mesh=mesh,
        in_specs=placed,
        out_specs=(P("ctx", "ch"), P("ch", "ctx")),
        check_vma=False,
    )
```

```python
import functools

import jax
import jax.numpy as jnp
from jax import lax
from jax.experimental import pallas as pl
from jax.experimental.pallas import tpu as pltpu
from jax.sharding import PartitionSpec as P

EXTRA = 8
VMEM = pltpu.VMEM


def pack_kernel(grad_ref, input_ref, filter_ref, out_ref, filter_vmem, sems):
    rows = grad_ref.shape[0]
    heads = filter_ref.shape[0]
    width = filter_ref.shape[1]
    copies = [
        pltpu.make_async_copy(filter_ref, filter_vmem, sems.at[0]),
        pltpu.make_async_copy(grad_ref, out_ref.at[pl.ds(0, rows)], sems.at[1]),
        pltpu.make_async_copy(input_ref, out_ref.at[pl.ds(rows, rows)], sems.at[2]),
    ]
    for copy in copies:
        copy.start()
    copies[0].wait()
    block = filter_vmem[...].astype(jnp.float32)
    block = jnp.concatenate([block, jnp.zeros((EXTRA - heads, width), jnp.float32)], axis=0)
    out_ref[2 * rows :, :width] = block.astype(out_ref.dtype)
    out_ref[2 * rows :, width:] = jnp.zeros((EXTRA, out_ref.shape[1] - width), out_ref.dtype)
    copies[1].wait()
    copies[2].wait()


def repeat(count, step, start):
    if count <= 4:
        for index in range(count):
            start = step(index, start)
        return start
    return lax.fori_loop(0, count, step, start)


def main_kernel(heads, factor, mine_ref, theirs_ref, out_ref, terms_ref, lags_ref, toeplitz_ref, out_vmem, terms_vmem, sems):
    half, span, channels = mine_ref.shape
    rows = (span - EXTRA) // 2
    width = channels // heads
    blocks = 2 * half
    position = lax.axis_index("ctx")
    pair = position // 2
    core = position - 2 * pair

    lags_ref[...] = jnp.zeros_like(lags_ref)

    def place(slot, carry):
        for ref, parity in ((mine_ref, core), (theirs_ref, 1 - core)):
            at = pl.multiple_of((blocks + 1 + 2 * slot + parity) * rows, rows)
            lags_ref[:, pl.ds(at, rows)] = ref[slot, 2 * rows :, :rows].astype(jnp.float32)
        return carry

    repeat(half, place, 0)
    start = pl.multiple_of((blocks - position) * rows, rows)
    window = lags_ref[:, pl.ds(start, (blocks + 1) * rows)]
    reach = (blocks + 1) * rows
    for head in range(heads):
        lines = jnp.broadcast_to(window[head : head + 1], (rows, reach))
        skewed = pltpu.roll(lines, 0, 1, stride=1, stride_axis=0)
        toeplitz_ref[head] = skewed[:, rows:].astype(toeplitz_ref.dtype)

    def compute(even_ref, odd_ref, parity):
        for head in range(heads):
            lanes = slice(head * width, (head + 1) * width)

            def accumulate(slot, total):
                both = jnp.concatenate([even_ref[slot, :rows, lanes], odd_ref[slot, :rows, lanes]], axis=0)
                at = slot * 2 * rows if isinstance(slot, int) else pl.multiple_of(slot * 2 * rows, 2 * rows)
                return total + jnp.dot(
                    toeplitz_ref[head, :, pl.ds(at, 2 * rows)], both, preferred_element_type=jnp.float32
                )

            total = repeat(half, accumulate, jnp.zeros((rows, width), jnp.float32))
            out_vmem[:, lanes] = (total * factor).astype(out_vmem.dtype)
            pltpu.make_async_copy(out_vmem.at[:, lanes], out_ref.at[:, lanes], sems.at[head]).start()

        sums = []
        for head in range(heads):
            lanes = slice(head * width, (head + 1) * width)

            def grad_at(ref, slot):
                held = ref[jnp.minimum(slot, half - 1), :rows, lanes]
                return jnp.where(slot < half, held, jnp.zeros_like(held))

            def accumulate(slot, total):
                mid = slot + pair
                if parity == 0:
                    first, second, third = grad_at(even_ref, mid), grad_at(odd_ref, mid), grad_at(even_ref, mid + 1)
                else:
                    first, second, third = grad_at(odd_ref, mid), grad_at(even_ref, mid + 1), grad_at(odd_ref, mid + 1)
                left = jnp.concatenate(
                    [even_ref[slot, rows : 2 * rows, lanes], odd_ref[slot, rows : 2 * rows, lanes]], axis=1
                )
                right = jnp.concatenate(
                    [jnp.concatenate([first, second], axis=1), jnp.concatenate([second, third], axis=1)], axis=0
                )
                return total + lax.dot_general(
                    left, right, (((1,), (1,)), ((), ())), preferred_element_type=jnp.float32
                )

            products = repeat(half, accumulate, jnp.zeros((rows, 2 * rows), jnp.float32))
            folded = products[0:8]
            for group in range(1, rows // 8):
                folded = folded + pltpu.roll(products[8 * group : 8 * group + 8], 2 * rows - 8 * group, 1)
            sums.append(folded)
        folded = jnp.concatenate(sums, axis=0)
        line = lax.broadcasted_iota(jnp.int32, folded.shape, 0)
        for bit in (1, 2, 4):
            folded = jnp.where((line & bit) != 0, pltpu.roll(folded, 2 * rows - bit, 1), folded)
        for head in range(heads):
            terms_vmem[head : head + 1, :] = (
                jnp.sum(folded[8 * head : 8 * head + 8, :rows], axis=0, keepdims=True) * factor
            )

    @pl.when(core == 0)
    def _():
        compute(mine_ref, theirs_ref, 0)

    @pl.when(core == 1)
    def _():
        compute(theirs_ref, mine_ref, 1)

    last = pltpu.make_async_copy(terms_vmem, terms_ref, sems.at[heads])
    last.start()
    for head in range(heads):
        lanes = slice(head * width, (head + 1) * width)
        pltpu.make_async_copy(out_vmem.at[:, lanes], out_ref.at[:, lanes], sems.at[head]).wait()
    last.wait()


def limit(size):
    return min(size + (4 << 20), 60 << 20)


def body(inputs, grad_out, filter_w):
    rows, channels = inputs.shape
    heads = filter_w.shape[0]
    blocks = lax.axis_size("ctx")
    half = blocks // 2
    factor = float(rows * blocks) ** (-0.5)
    anywhere = pl.BlockSpec(memory_space=pl.ANY)
    on_chip = pl.BlockSpec(memory_space=VMEM)
    span = 2 * rows + EXTRA
    payload = pl.pallas_call(
        pack_kernel,
        out_shape=jax.ShapeDtypeStruct((span, channels), inputs.dtype),
        in_specs=[pl.BlockSpec(memory_space=pltpu.HBM)] * 3,
        out_specs=on_chip,
        scratch_shapes=[VMEM(filter_w.shape, filter_w.dtype), pltpu.SemaphoreType.DMA((3,))],
        compiler_params=pltpu.CompilerParams(vmem_limit_bytes=limit(3 * span * channels * 2)),
        name="pack",
    )(*(pltpu.with_memory_space_constraint(each, pltpu.HBM) for each in (grad_out, inputs, filter_w)))
    scratch = 4 * EXTRA * (2 * blocks + 1) * rows + 2 * heads * rows * blocks * rows + 8 * rows * channels
    groups = [[2 * slot + core for slot in range(half)] for core in range(2)]
    mine = lax.all_gather(payload, "ctx", axis=0, tiled=False, axis_index_groups=groups)
    theirs = lax.ppermute(mine, "ctx", [(index, index ^ 1) for index in range(blocks)])
    return pl.pallas_call(
        functools.partial(main_kernel, heads, factor),
        out_shape=(
            jax.ShapeDtypeStruct((rows, channels), inputs.dtype),
            jax.ShapeDtypeStruct((heads, rows), jnp.float32),
        ),
        in_specs=[on_chip] * 2,
        out_specs=(anywhere, anywhere),
        scratch_shapes=[
            VMEM((EXTRA, (2 * blocks + 1) * rows), jnp.float32),
            VMEM((heads, rows, blocks * rows), inputs.dtype),
            VMEM((rows, channels), inputs.dtype),
            VMEM((heads, rows), jnp.float32),
            pltpu.SemaphoreType.DMA((heads + 1,)),
        ],
        compiler_params=pltpu.CompilerParams(vmem_limit_bytes=limit(scratch)),
        name="main",
    )(mine, theirs)


def solution(mesh):
    placed = (P("ctx", "ch"), P("ctx", "ch"), P("ch", "ctx"))
    return jax.shard_map(
        body,
        mesh=mesh,
        in_specs=placed,
        out_specs=(P("ctx", "ch"), P("ch", "ctx")),
        check_vma=False,
    )
```

```python
import functools

import jax
import jax.numpy as jnp
from jax import lax
from jax.experimental import pallas as pl
from jax.experimental.pallas import tpu as pltpu
from jax.sharding import PartitionSpec as P

EXTRA = 8
VMEM = pltpu.VMEM
ANYWHERE = pl.BlockSpec(memory_space=pl.ANY)
ON_CHIP = pl.BlockSpec(memory_space=VMEM)


def pack_kernel(grad_ref, input_ref, filter_ref, out_ref, filter_vmem, sems):
    rows = grad_ref.shape[0]
    heads, width = filter_ref.shape
    copies = [
        pltpu.make_async_copy(filter_ref, filter_vmem, sems.at[0]),
        pltpu.make_async_copy(grad_ref, out_ref.at[pl.ds(0, rows)], sems.at[1]),
        pltpu.make_async_copy(input_ref, out_ref.at[pl.ds(rows + EXTRA, rows)], sems.at[2]),
    ]
    for copy in copies:
        copy.start()
    copies[0].wait()
    block = filter_vmem[...].astype(jnp.float32)
    block = jnp.concatenate([block, jnp.zeros((EXTRA - heads, width), jnp.float32)], axis=0)
    lags = slice(rows, rows + EXTRA)
    out_ref[lags, :width] = block.astype(out_ref.dtype)
    out_ref[lags, width:] = jnp.zeros((EXTRA, out_ref.shape[1] - width), out_ref.dtype)
    copies[1].wait()
    copies[2].wait()


def repeat(count, step, start):
    if count <= 4:
        for index in range(count):
            start = step(index, start)
        return start
    return lax.fori_loop(0, count, step, start)


def place_in_axis():
    position = lax.axis_index("ctx")
    pair = position // 2
    return position, pair, position - 2 * pair


def lanes_of(head, width):
    return slice(head * width, (head + 1) * width)


def run_of(half):
    return 2 if half % 2 == 0 else 1


def side_by_side(ref, slot, half, rows, lanes):
    return jnp.concatenate([ref[slot + step, rows, lanes] for step in range(run_of(half))], axis=1)


def later(ref, slot, half, rows, lanes):
    parts = []
    for step in range(run_of(half)):
        at = slot + step
        held = ref[jnp.minimum(at, half - 1), rows, lanes]
        parts.append(jnp.where(at < half, held, jnp.zeros_like(held)))
    return jnp.concatenate(parts, axis=1)


def times(left, right):
    return lax.dot_general(left, right, (((1,), (1,)), ((), ())), preferred_element_type=jnp.float32)


def own_kernel(heads, mine_ref, even_ref):
    half, span, channels = mine_ref.shape
    rows = (span - EXTRA) // 2
    width = channels // heads
    _, pair, core = place_in_axis()
    grads, inputs = slice(0, rows), slice(rows + EXTRA, span)
    for head in range(heads):
        lanes = lanes_of(head, width)

        def step(index, total):
            slot = index * run_of(half)
            left = side_by_side(mine_ref, slot, half, inputs, lanes)
            return total + times(left, later(mine_ref, slot + pair + core, half, grads, lanes))

        even_ref[head] = repeat(half // run_of(half), step, jnp.zeros((rows, rows), jnp.float32))


def toeplitz_kernel(heads, mine_ref, grad_ref, toeplitz_ref, lags_ref):
    half, span, _ = mine_ref.shape
    rows = (span - EXTRA) // 2
    blocks = 2 * half
    position, _, core = place_in_axis()
    lags_ref[:, : (blocks + 1) * rows] = jnp.zeros((EXTRA, (blocks + 1) * rows), jnp.float32)

    def place(slot, carry):
        for ref, parity in ((mine_ref, core), (grad_ref, 1 - core)):
            held = ref[slot, rows : rows + EXTRA, :rows]
            at = pl.multiple_of((blocks + 1 + 2 * slot + parity) * rows, rows)
            lags_ref[:, pl.ds(at, rows)] = held.astype(jnp.float32)
        return carry

    repeat(half, place, 0)
    reach = (blocks + 1) * rows
    start = pl.multiple_of((blocks - position) * rows, rows)
    window = lags_ref[:, pl.ds(start, reach)]
    for head in range(heads):
        lines = jnp.broadcast_to(window[head : head + 1], (rows, reach))
        skewed = pltpu.roll(lines, 0, 1, stride=1, stride_axis=0)
        toeplitz_ref[head] = skewed[:, rows:].astype(toeplitz_ref.dtype)


def input_kernel(heads, factor, mine_ref, grad_ref, toeplitz_ref, out_ref, odd_ref):
    half, span, channels = mine_ref.shape
    rows = (span - EXTRA) // 2
    width = channels // heads
    _, pair, core = place_in_axis()
    grads, inputs = slice(0, rows), slice(rows + EXTRA, span)
    for head in range(heads):
        lanes = lanes_of(head, width)

        def gather(slot, total):
            own = pl.multiple_of((2 * slot + core) * rows, rows)
            other = pl.multiple_of((2 * slot + 1 - core) * rows, rows)
            left = jnp.concatenate(
                [toeplitz_ref[head, :, pl.ds(own, rows)], toeplitz_ref[head, :, pl.ds(other, rows)]], axis=1
            )
            both = jnp.concatenate([mine_ref[slot, grads, lanes], grad_ref[slot, grads, lanes]], axis=0)
            return total + jnp.dot(left, both, preferred_element_type=jnp.float32)

        total = repeat(half, gather, jnp.zeros((rows, width), jnp.float32))
        out_ref[:, lanes] = (total * factor).astype(out_ref.dtype)
    for head in range(heads):
        lanes = lanes_of(head, width)

        def step(index, total):
            slot = index * run_of(half)
            left = side_by_side(mine_ref, slot, half, inputs, lanes)
            return total + times(left, later(grad_ref, slot + pair + core, half, grads, lanes))

        odd_ref[head] = repeat(half // run_of(half), step, jnp.zeros((rows, rows), jnp.float32))


def filter_kernel(
    heads, factor, mine_ref, grad_ref, input_ref, even_ref, odd_ref, held_ref, out_ref, terms_ref, terms_vmem, sems
):
    half, rows, channels = input_ref.shape
    width = channels // heads
    _, pair, core = place_in_axis()
    output = pltpu.make_async_copy(held_ref, out_ref, sems.at[0])
    output.start()
    whole = slice(0, rows)
    sums = []
    for head in range(heads):
        lanes = lanes_of(head, width)

        def step(index, total):
            slot = index * run_of(half)
            left = side_by_side(input_ref, slot, half, whole, lanes)
            right = jnp.concatenate(
                [
                    later(grad_ref, slot + pair + core, half, whole, lanes),
                    later(mine_ref, slot + pair + 1 - core, half, whole, lanes),
                ],
                axis=0,
            )
            return total + times(left, right)

        products = repeat(half // run_of(half), step, jnp.zeros((rows, 2 * rows), jnp.float32))
        even = products[:, :rows] + even_ref[head]
        odd = products[:, rows:] + odd_ref[head]
        products = jnp.concatenate([jnp.where(core == 0, even, odd), jnp.where(core == 0, odd, even)], axis=1)
        folded = products[0:8]
        for group in range(1, rows // 8):
            folded = folded + pltpu.roll(products[8 * group : 8 * group + 8], 2 * rows - 8 * group, 1)
        sums.append(folded)
    folded = jnp.concatenate(sums, axis=0)
    line = lax.broadcasted_iota(jnp.int32, folded.shape, 0)
    for bit in (1, 2, 4):
        folded = jnp.where((line & bit) != 0, pltpu.roll(folded, 2 * rows - bit, 1), folded)
    for head in range(heads):
        terms_vmem[head : head + 1, :] = jnp.sum(folded[8 * head : 8 * head + 8, :rows], axis=0, keepdims=True) * factor
    terms = pltpu.make_async_copy(terms_vmem, terms_ref, sems.at[1])
    terms.start()
    output.wait()
    terms.wait()


def call(kernel, name, args, out_shape, out_specs, scratch=(), scratch_bytes=0, in_specs=None, micros=1.0):
    return pl.pallas_call(
        kernel,
        out_shape=out_shape,
        in_specs=in_specs or [ON_CHIP] * len(args),
        out_specs=out_specs,
        scratch_shapes=list(scratch),
        compiler_params=pltpu.CompilerParams(vmem_limit_bytes=min(scratch_bytes + (4 << 20), 60 << 20)),
        cost_estimate=pl.CostEstimate(flops=int(micros * 1e9), bytes_accessed=int(micros * 3e6), transcendentals=0),
        name=name,
    )(*args)


def body(inputs, grad_out, filter_w):
    rows, channels = inputs.shape
    heads = filter_w.shape[0]
    blocks = lax.axis_size("ctx")
    half = blocks // 2
    factor = float(rows * blocks) ** (-0.5)
    kind = inputs.dtype
    span = 2 * rows + EXTRA
    shape = jax.ShapeDtypeStruct
    swaps = [(index, index ^ 1) for index in range(blocks)]
    payload = call(
        pack_kernel,
        "pack",
        [pltpu.with_memory_space_constraint(each, pltpu.HBM) for each in (grad_out, inputs, filter_w)],
        shape((span, channels), kind),
        ON_CHIP,
        [VMEM(filter_w.shape, filter_w.dtype), pltpu.SemaphoreType.DMA((3,))],
        in_specs=[pl.BlockSpec(memory_space=pltpu.HBM)] * 3,
    )
    groups = [[2 * slot + core for slot in range(half)] for core in range(2)]
    mine = lax.all_gather(payload, "ctx", axis=0, tiled=False, axis_index_groups=groups)
    grads = lax.ppermute(mine[:, : rows + EXTRA], "ctx", swaps)
    others = lax.ppermute(mine[:, rows + EXTRA :], "ctx", swaps)
    square = shape((heads, rows, rows), jnp.float32)
    even = call(functools.partial(own_kernel, heads), "own", [mine], square, ON_CHIP)
    toeplitz = call(
        functools.partial(toeplitz_kernel, heads),
        "toeplitz",
        [mine, grads],
        shape((heads, rows, blocks * rows), kind),
        ON_CHIP,
        [VMEM((EXTRA, (2 * blocks + 1) * rows), jnp.float32)],
        4 * EXTRA * (2 * blocks + 1) * rows,
    )
    held, odd = call(
        functools.partial(input_kernel, heads, factor),
        "input",
        [mine, grads, toeplitz],
        (shape((rows, channels), kind), square),
        (ON_CHIP, ON_CHIP),
    )
    return call(
        functools.partial(filter_kernel, heads, factor),
        "filter",
        [mine, grads, others, even, odd, held],
        (shape((rows, channels), kind), shape((heads, rows), jnp.float32)),
        (ANYWHERE, ANYWHERE),
        [VMEM((heads, rows), jnp.float32), pltpu.SemaphoreType.DMA((2,))],
    )


def solution(mesh):
    placed = (P("ctx", "ch"), P("ctx", "ch"), P("ch", "ctx"))
    return jax.shard_map(
        body,
        mesh=mesh,
        in_specs=placed,
        out_specs=(P("ctx", "ch"), P("ch", "ctx")),
        check_vma=False,
    )
```

```python
import functools

import jax
import jax.numpy as jnp
from jax import lax
from jax.experimental import pallas as pl
from jax.experimental.pallas import tpu as pltpu
from jax.sharding import PartitionSpec as P


EXTRA = 8
PIECES = 2
VMEM = pltpu.VMEM
ANYWHERE = pl.BlockSpec(memory_space=pl.ANY)
ON_CHIP = pl.BlockSpec(memory_space=VMEM)


def pack_kernel(grad_ref, input_ref, filter_ref, out_ref, filter_vmem, sems):
    rows = grad_ref.shape[0]
    heads, width = filter_ref.shape
    copies = [pltpu.make_async_copy(filter_ref, filter_vmem, sems.at[0])]
    piece = rows // PIECES
    for at in range(PIECES):
        part = pl.ds(at * piece, piece)
        copies.append(pltpu.make_async_copy(grad_ref.at[part], out_ref.at[part], sems.at[1 + 2 * at]))
        into = pl.ds(rows + EXTRA + at * piece, piece)
        copies.append(pltpu.make_async_copy(input_ref.at[part], out_ref.at[into], sems.at[2 + 2 * at]))
    for copy in copies:
        copy.start()
    copies[0].wait()
    block = filter_vmem[...].astype(jnp.float32)
    block = jnp.concatenate([block, jnp.zeros((EXTRA - heads, width), jnp.float32)], axis=0)
    lags = slice(rows, rows + EXTRA)
    out_ref[lags, :width] = block.astype(out_ref.dtype)
    out_ref[lags, width:] = jnp.zeros((EXTRA, out_ref.shape[1] - width), out_ref.dtype)
    for copy in copies[1:]:
        copy.wait()


def repeat(count, step, start):
    if count <= 4:
        for index in range(count):
            start = step(index, start)
        return start
    return lax.fori_loop(0, count, step, start)


def place_in_axis():
    position = lax.axis_index("ctx")
    pair = position // 2
    return position, pair, position - 2 * pair


def lanes_of(head, width):
    return slice(head * width, (head + 1) * width)


def run_of(half):
    return next(run for run in (4, 2, 1) if half % run == 0)


def side_by_side(ref, slot, half, rows, lanes):
    return jnp.concatenate([ref[slot + step, rows, lanes] for step in range(run_of(half))], axis=1)


def later(ref, slot, half, rows, lanes):
    parts = []
    for step in range(run_of(half)):
        at = slot + step
        held = ref[jnp.minimum(at, half - 1), rows, lanes]
        parts.append(jnp.where(at < half, held, jnp.zeros_like(held)))
    return jnp.concatenate(parts, axis=1)


def times(left, right):
    return lax.dot_general(left, right, (((1,), (1,)), ((), ())), preferred_element_type=jnp.float32)


def own_kernel(heads, mine_ref, even_ref):
    half, span, channels = mine_ref.shape
    rows = (span - EXTRA) // 2
    width = channels // heads
    _, pair, core = place_in_axis()
    grads, inputs = slice(0, rows), slice(rows + EXTRA, span)
    for head in range(heads):
        lanes = lanes_of(head, width)

        def step(index, total):
            slot = index * run_of(half)
            left = side_by_side(mine_ref, slot, half, inputs, lanes)
            return total + times(left, later(mine_ref, slot + pair + core, half, grads, lanes))

        even_ref[head] = repeat(half // run_of(half), step, jnp.zeros((rows, rows), jnp.float32))


def toeplitz_kernel(heads, mine_ref, filter_ref, toeplitz_ref, lags_ref):
    half, span, _ = mine_ref.shape
    rows = (span - EXTRA) // 2
    blocks = 2 * half
    position, _, core = place_in_axis()
    lags_ref[:, : (blocks + 1) * rows] = jnp.zeros((EXTRA, (blocks + 1) * rows), jnp.float32)

    def place(slot, carry):
        for held, parity in ((mine_ref[slot, rows : rows + EXTRA, :rows], core), (filter_ref[slot], 1 - core)):
            at = pl.multiple_of((blocks + 1 + 2 * slot + parity) * rows, rows)
            lags_ref[:, pl.ds(at, rows)] = held.astype(jnp.float32)
        return carry

    repeat(half, place, 0)
    reach = (blocks + 1) * rows
    start = pl.multiple_of((blocks - position) * rows, rows)
    window = lags_ref[:, pl.ds(start, reach)]
    for head in range(heads):
        lines = jnp.broadcast_to(window[head : head + 1], (rows, reach)).astype(toeplitz_ref.dtype)
        skewed = pltpu.roll(lines, 0, 1, stride=1, stride_axis=0)
        toeplitz_ref[head] = skewed[:, rows:]


def input_kernel(heads, factor, mine_ref, grad_ref, toeplitz_ref, out_ref, odd_ref):
    half, span, channels = mine_ref.shape
    rows = (span - EXTRA) // 2
    width = channels // heads
    _, pair, core = place_in_axis()
    grads, inputs = slice(0, rows), slice(rows + EXTRA, span)
    for head in range(heads):
        lanes = lanes_of(head, width)

        def gather(slot, total):
            own = pl.multiple_of((2 * slot + core) * rows, rows)
            other = pl.multiple_of((2 * slot + 1 - core) * rows, rows)
            left = jnp.concatenate(
                [toeplitz_ref[head, :, pl.ds(own, rows)], toeplitz_ref[head, :, pl.ds(other, rows)]], axis=1
            )
            both = jnp.concatenate([mine_ref[slot, grads, lanes], grad_ref[slot, grads, lanes]], axis=0)
            return total + jnp.dot(left, both, preferred_element_type=jnp.float32)

        total = repeat(half, gather, jnp.zeros((rows, width), jnp.float32))
        out_ref[:, lanes] = (total * factor).astype(out_ref.dtype)
    for head in range(heads):
        lanes = lanes_of(head, width)

        def step(index, total):
            slot = index * run_of(half)
            left = side_by_side(mine_ref, slot, half, inputs, lanes)
            return total + times(left, later(grad_ref, slot + pair + core, half, grads, lanes))

        odd_ref[head] = repeat(half // run_of(half), step, jnp.zeros((rows, rows), jnp.float32))


def filter_kernel(
    heads, factor, mine_ref, grad_ref, input_ref, even_ref, odd_ref, held_ref, out_ref, terms_ref, terms_vmem, sems
):
    half, rows, channels = input_ref.shape
    width = channels // heads
    _, pair, core = place_in_axis()
    output = pltpu.make_async_copy(held_ref, out_ref, sems.at[0])
    output.start()
    whole = slice(0, rows)
    sums = []
    for head in range(heads):
        lanes = lanes_of(head, width)

        def step(index, total):
            slot = index * run_of(half)
            left = side_by_side(input_ref, slot, half, whole, lanes)
            right = jnp.concatenate(
                [
                    later(grad_ref, slot + pair + core, half, whole, lanes),
                    later(mine_ref, slot + pair + 1 - core, half, whole, lanes),
                ],
                axis=0,
            )
            return total + times(left, right)

        products = repeat(half // run_of(half), step, jnp.zeros((rows, 2 * rows), jnp.float32))
        even = products[:, :rows] + even_ref[head]
        odd = products[:, rows:] + odd_ref[head]
        products = jnp.concatenate([jnp.where(core == 0, even, odd), jnp.where(core == 0, odd, even)], axis=1)
        folded = products[0:8]
        for group in range(1, rows // 8):
            folded = folded + pltpu.roll(products[8 * group : 8 * group + 8], 2 * rows - 8 * group, 1)
        sums.append(folded)
    folded = jnp.concatenate(sums, axis=0)
    line = lax.broadcasted_iota(jnp.int32, folded.shape, 0) & 7
    terms = jnp.where(line == 0, folded, 0.0)
    for shift in range(1, 8):
        terms = terms + jnp.where(line == shift, pltpu.roll(folded, 2 * rows - shift, 1), 0.0)
    for head in range(heads):
        terms_vmem[head : head + 1, :] = jnp.sum(terms[8 * head : 8 * head + 8, :rows], axis=0, keepdims=True) * factor
    last = pltpu.make_async_copy(terms_vmem, terms_ref, sems.at[1])
    last.start()
    output.wait()
    last.wait()


def call(kernel, args, out_shape, out_specs, scratch=(), scratch_bytes=0, in_specs=None, micros=1.0):
    return pl.pallas_call(
        kernel,
        out_shape=out_shape,
        in_specs=in_specs or [ON_CHIP] * len(args),
        out_specs=out_specs,
        scratch_shapes=list(scratch),
        compiler_params=pltpu.CompilerParams(vmem_limit_bytes=min(scratch_bytes + (4 << 20), 60 << 20)),
        cost_estimate=pl.CostEstimate(flops=int(micros * 1e9), bytes_accessed=int(micros * 3e6), transcendentals=0),
    )(*args)


def body(inputs, grad_out, filter_w):
    rows, channels = inputs.shape
    heads = filter_w.shape[0]
    blocks = lax.axis_size("ctx")
    half = blocks // 2
    factor = float(rows * blocks) ** (-0.5)
    kind = inputs.dtype
    span = 2 * rows + EXTRA
    shape = jax.ShapeDtypeStruct
    swaps = [(index, index ^ 1) for index in range(blocks)]
    payload = call(
        pack_kernel,
        [pltpu.with_memory_space_constraint(each, pltpu.HBM) for each in (grad_out, inputs, filter_w)],
        shape((span, channels), kind),
        ON_CHIP,
        [VMEM(filter_w.shape, filter_w.dtype), pltpu.SemaphoreType.DMA((1 + 2 * PIECES,))],
        in_specs=[pl.BlockSpec(memory_space=pltpu.HBM)] * 3,
    )
    groups = [[2 * slot + core for slot in range(half)] for core in range(2)]
    mine = lax.all_gather(payload, "ctx", axis=0, tiled=False, axis_index_groups=groups)
    filters = lax.ppermute(mine[:, rows : rows + EXTRA, :rows], "ctx", swaps)
    grads = lax.ppermute(mine[:, :rows], "ctx", swaps)
    others = lax.ppermute(mine[:, rows + EXTRA :], "ctx", swaps)
    square = shape((heads, rows, rows), jnp.float32)
    even = call(functools.partial(own_kernel, heads), [mine], square, ON_CHIP)
    toeplitz = call(
        functools.partial(toeplitz_kernel, heads),
        [mine, filters],
        shape((heads, rows, blocks * rows), kind),
        ON_CHIP,
        [VMEM((EXTRA, (2 * blocks + 1) * rows), jnp.float32)],
        4 * EXTRA * (2 * blocks + 1) * rows,
    )
    held, odd = call(
        functools.partial(input_kernel, heads, factor),
        [mine, grads, toeplitz],
        (shape((rows, channels), kind), square),
        (ON_CHIP, ON_CHIP),
    )
    return call(
        functools.partial(filter_kernel, heads, factor),
        [mine, grads, others, even, odd, held],
        (shape((rows, channels), kind), shape((heads, rows), jnp.float32)),
        (ANYWHERE, ANYWHERE),
        [VMEM((heads, rows), jnp.float32), pltpu.SemaphoreType.DMA((2,))],
    )


def solution(mesh):
    placed = (P("ctx", "ch"), P("ctx", "ch"), P("ch", "ctx"))
    return jax.shard_map(
        body,
        mesh=mesh,
        in_specs=placed,
        out_specs=(P("ctx", "ch"), P("ch", "ctx")),
        check_vma=False,
    )
```

```python
import functools

import jax
import jax.numpy as jnp
from jax import lax
from jax.experimental import pallas as pl
from jax.experimental.pallas import tpu as pltpu
from jax.sharding import PartitionSpec as P


EXTRA = 8
VMEM = pltpu.VMEM
ANYWHERE = pl.BlockSpec(memory_space=pl.ANY)
ON_CHIP = pl.BlockSpec(memory_space=VMEM)


def pack_kernel(grad_ref, input_ref, filter_ref, out_ref, filter_vmem, sems):
    rows = grad_ref.shape[0]
    heads, width = filter_ref.shape
    base = heads * rows + EXTRA
    copies = [pltpu.make_async_copy(filter_ref, filter_vmem, sems.at[0])]
    for head in range(heads):
        lanes = pl.ds(head * width, width)
        for ref, start, nth in ((grad_ref, EXTRA, 1), (input_ref, base, 2)):
            into = out_ref.at[pl.ds(start + head * rows, rows)]
            copies.append(pltpu.make_async_copy(ref.at[:, lanes], into, sems.at[2 * head + nth]))
    for copy in copies:
        copy.start()
    copies[0].wait()
    block = filter_vmem[...].astype(jnp.float32)
    block = jnp.concatenate([block, jnp.zeros((EXTRA - heads, width), jnp.float32)], axis=0)
    out_ref[:EXTRA, :] = block.astype(out_ref.dtype)
    for copy in copies[1:]:
        copy.wait()


def repeat(count, step, start):
    if count <= 4:
        for index in range(count):
            start = step(index, start)
        return start
    return lax.fori_loop(0, count, step, start)


def place_in_axis():
    position = lax.axis_index("ctx")
    pair = position // 2
    return position, pair, position - 2 * pair


def rows_of(head, rows, base=0):
    return slice(base + head * rows, base + (head + 1) * rows)


def run_of(half):
    return next(run for run in (4, 2, 1) if half % run == 0)


def side_by_side(ref, slot, half, lines):
    return jnp.concatenate([ref[slot + step, lines, :] for step in range(run_of(half))], axis=1)


def later(ref, slot, half, lines):
    parts = []
    for step in range(run_of(half)):
        at = slot + step
        held = ref[jnp.minimum(at, half - 1), lines, :]
        parts.append(jnp.where(at < half, held, jnp.zeros_like(held)))
    return jnp.concatenate(parts, axis=1)


def times(left, right):
    return lax.dot_general(left, right, (((1,), (1,)), ((), ())), preferred_element_type=jnp.float32)


def own_kernel(heads, mine_ref, even_ref, shifted_ref):
    half, span, _ = mine_ref.shape
    rows = (span - EXTRA) // (2 * heads)
    base = heads * rows + EXTRA
    _, pair, core = place_in_axis()
    for head in range(heads):

        def step(index, total):
            slot = index * run_of(half)
            left = side_by_side(mine_ref, slot, half, rows_of(head, rows, base))
            return total + times(left, later(mine_ref, slot + pair + core, half, rows_of(head, rows, EXTRA)))

        even_ref[head] = repeat(half // run_of(half), step, jnp.zeros((rows, rows), jnp.float32))

    def shift(slot, carry):
        at = slot + pair + 1 - core
        held = mine_ref[jnp.minimum(at, half - 1), EXTRA : EXTRA + heads * rows, :]
        shifted_ref[slot] = jnp.where(at < half, held, jnp.zeros_like(held))
        return carry

    repeat(half, shift, 0)


def toeplitz_kernel(heads, mine_ref, lead_ref, toeplitz_ref, lags_ref):
    half, span, _ = mine_ref.shape
    rows = (span - EXTRA) // (2 * heads)
    blocks = 2 * half
    position, _, core = place_in_axis()
    lags_ref[:, : (blocks + 1) * rows] = jnp.zeros((EXTRA, (blocks + 1) * rows), jnp.float32)

    def place(slot, carry):
        for held, parity in ((mine_ref[slot, :EXTRA, :], core), (lead_ref[slot, :EXTRA, :], 1 - core)):
            at = pl.multiple_of((blocks + 1 + 2 * slot + parity) * rows, rows)
            lags_ref[:, pl.ds(at, rows)] = held.astype(jnp.float32)
        return carry

    repeat(half, place, 0)
    reach = (blocks + 1) * rows
    start = pl.multiple_of((blocks - position) * rows, rows)
    window = lags_ref[:, pl.ds(start, reach)]
    for head in range(heads):
        lines = jnp.broadcast_to(window[head : head + 1], (rows, reach)).astype(toeplitz_ref.dtype)
        skewed = pltpu.roll(lines, 0, 1, stride=1, stride_axis=0)
        toeplitz_ref[head] = skewed[:, rows:]


def input_kernel(heads, factor, mine_ref, lead_ref, rest_ref, toeplitz_ref, out_ref, odd_ref, shifted_ref):
    half, span, width = mine_ref.shape
    rows = (span - EXTRA) // (2 * heads)
    base = heads * rows + EXTRA
    lead = (lead_ref.shape[1] - EXTRA) // rows
    _, pair, core = place_in_axis()

    def theirs(head):
        return (lead_ref, rows_of(head, rows, EXTRA)) if head < lead else (rest_ref, rows_of(head - lead, rows))

    for head in range(heads):
        lines = rows_of(head, rows, EXTRA)
        grad_ref, others = theirs(head)

        def gather(index, total):
            left, right = [], []
            for nth in range(run_of(half)):
                slot = index * run_of(half) + nth
                for at, block in ((2 * slot + core, mine_ref[slot, lines, :]), (2 * slot + 1 - core, grad_ref[slot, others, :])):
                    left.append(toeplitz_ref[head, :, pl.ds(pl.multiple_of(at * rows, rows), rows)])
                    right.append(block)
            return total + jnp.dot(
                jnp.concatenate(left, axis=1), jnp.concatenate(right, axis=0), preferred_element_type=jnp.float32
            )

        total = repeat(half // run_of(half), gather, jnp.zeros((rows, width), jnp.float32))
        out_ref[:, head * width : (head + 1) * width] = (total * factor).astype(out_ref.dtype)
    for head in range(heads):
        grad_ref, others = theirs(head)

        def step(index, total):
            slot = index * run_of(half)
            left = side_by_side(mine_ref, slot, half, rows_of(head, rows, base))
            right = later(grad_ref, slot + pair + core, half, others)
            for nth in range(run_of(half)):
                shifted_ref[slot + nth, rows_of(head, rows), :] = right[:, nth * width : (nth + 1) * width]
            return total + times(left, right)

        odd_ref[head] = repeat(half // run_of(half), step, jnp.zeros((rows, rows), jnp.float32))


def filter_kernel(
    heads, factor, own_ref, other_ref, input_ref, even_ref, odd_ref, held_ref, out_ref, terms_ref, terms_vmem, sems
):
    half, lines, _ = input_ref.shape
    rows = lines // heads
    _, _, core = place_in_axis()
    output = pltpu.make_async_copy(held_ref, out_ref, sems.at[0])
    output.start()
    source = lax.broadcasted_iota(jnp.int32, (rows, rows), 0)
    target = lax.broadcasted_iota(jnp.int32, (rows, rows), 1)
    first = (target >= source) == (core == 0)
    sums = []
    for head in range(heads):
        lines = rows_of(head, rows)

        def step(index, total):
            slot = index * run_of(half)
            left = side_by_side(input_ref, slot, half, lines)
            right = jnp.concatenate(
                [side_by_side(other_ref, slot, half, lines), side_by_side(own_ref, slot, half, lines)], axis=0
            )
            return total + times(left, right)

        products = repeat(half // run_of(half), step, jnp.zeros((rows, 2 * rows), jnp.float32))
        even = products[:, :rows] + even_ref[head]
        odd = products[:, rows:] + odd_ref[head]
        terms = jnp.where(first, even, odd)
        folded = terms[0:8]
        for group in range(1, rows // 8):
            folded = folded + pltpu.roll(terms[8 * group : 8 * group + 8], rows - 8 * group, 1)
        sums.append(folded)
    folded = jnp.concatenate(sums, axis=0)
    line = lax.broadcasted_iota(jnp.int32, folded.shape, 0) & 7
    terms = jnp.where(line == 0, folded, 0.0)
    for shift in range(1, 8):
        terms = terms + jnp.where(line == shift, pltpu.roll(folded, rows - shift, 1), 0.0)
    for head in range(heads):
        terms_vmem[head : head + 1, :] = jnp.sum(terms[8 * head : 8 * head + 8], axis=0, keepdims=True) * factor
    last = pltpu.make_async_copy(terms_vmem, terms_ref, sems.at[1])
    last.start()
    output.wait()
    last.wait()


def call(kernel, args, out_shape, out_specs, scratch=(), scratch_bytes=0, in_specs=None, micros=1.0):
    return pl.pallas_call(
        kernel,
        out_shape=out_shape,
        in_specs=in_specs or [ON_CHIP] * len(args),
        out_specs=out_specs,
        scratch_shapes=list(scratch),
        compiler_params=pltpu.CompilerParams(vmem_limit_bytes=min(scratch_bytes + (4 << 20), 60 << 20)),
        cost_estimate=pl.CostEstimate(flops=int(micros * 1e9), bytes_accessed=int(micros * 3e6), transcendentals=0),
    )(*args)


def body(inputs, grad_out, filter_w):
    rows, channels = inputs.shape
    heads = filter_w.shape[0]
    blocks = lax.axis_size("ctx")
    half = blocks // 2
    factor = float(rows * blocks) ** (-0.5)
    kind = inputs.dtype
    width = channels // heads
    base = heads * rows + EXTRA
    span = base + heads * rows
    shape = jax.ShapeDtypeStruct
    swaps = [(index, index ^ 1) for index in range(blocks)]
    payload = call(
        pack_kernel,
        [pltpu.with_memory_space_constraint(each, pltpu.HBM) for each in (grad_out, inputs, filter_w)],
        shape((span, width), kind),
        ON_CHIP,
        [VMEM(filter_w.shape, filter_w.dtype), pltpu.SemaphoreType.DMA((1 + 2 * heads,))],
        in_specs=[pl.BlockSpec(memory_space=pltpu.HBM)] * 3,
    )
    groups = [[2 * slot + core for slot in range(half)] for core in range(2)]
    mine = lax.all_gather(payload, "ctx", axis=0, tiled=False, axis_index_groups=groups)
    cut = EXTRA + rows
    lead = lax.ppermute(mine[:, :cut], "ctx", swaps)
    rest = lax.ppermute(mine[:, cut:base], "ctx", swaps)
    others = lax.ppermute(mine[:, base:], "ctx", swaps)
    square = shape((heads, rows, rows), jnp.float32)
    shifted = shape((half, heads * rows, width), kind)
    even, own = call(functools.partial(own_kernel, heads), [mine], (square, shifted), (ON_CHIP, ON_CHIP))
    toeplitz = call(
        functools.partial(toeplitz_kernel, heads),
        [mine, lead],
        shape((heads, rows, blocks * rows), kind),
        ON_CHIP,
        [VMEM((EXTRA, (2 * blocks + 1) * rows), jnp.float32)],
        4 * EXTRA * (2 * blocks + 1) * rows,
    )
    held, odd, other = call(
        functools.partial(input_kernel, heads, factor),
        [mine, lead, rest, toeplitz],
        (shape((rows, channels), kind), square, shifted),
        (ON_CHIP, ON_CHIP, ON_CHIP),
    )
    return call(
        functools.partial(filter_kernel, heads, factor),
        [own, other, others, even, odd, held],
        (shape((rows, channels), kind), shape((heads, rows), jnp.float32)),
        (ANYWHERE, ANYWHERE),
        [VMEM((heads, rows), jnp.float32), pltpu.SemaphoreType.DMA((2,))],
    )


def solution(mesh):
    placed = (P("ctx", "ch"), P("ctx", "ch"), P("ch", "ctx"))
    return jax.shard_map(
        body,
        mesh=mesh,
        in_specs=placed,
        out_specs=(P("ctx", "ch"), P("ch", "ctx")),
        check_vma=False,
    )
```

```python
import functools

import jax
import jax.numpy as jnp
from jax import lax
from jax.experimental import pallas as pl
from jax.experimental.pallas import tpu as pltpu
from jax.sharding import PartitionSpec as P


EXTRA = 8
VMEM = pltpu.VMEM
ANYWHERE = pl.BlockSpec(memory_space=pl.ANY)
ON_CHIP = pl.BlockSpec(memory_space=VMEM)


def pack_kernel(grad_ref, input_ref, filter_ref, out_ref, filter_vmem, sems):
    rows = grad_ref.shape[0]
    heads, width = filter_ref.shape
    base = heads * rows + EXTRA
    copies = [pltpu.make_async_copy(filter_ref, filter_vmem, sems.at[0])]
    for head in range(heads):
        lanes = pl.ds(head * width, width)
        for ref, start, nth in ((grad_ref, EXTRA, 1), (input_ref, base, 2)):
            into = out_ref.at[pl.ds(start + head * rows, rows)]
            copies.append(pltpu.make_async_copy(ref.at[:, lanes], into, sems.at[2 * head + nth]))
    for copy in copies:
        copy.start()
    copies[0].wait()
    block = filter_vmem[...].astype(jnp.float32)
    block = jnp.concatenate([block, jnp.zeros((EXTRA - heads, width), jnp.float32)], axis=0)
    out_ref[:EXTRA, :] = block.astype(out_ref.dtype)
    for copy in copies[1:]:
        copy.wait()


def repeat(count, step, start):
    if count <= 4:
        for index in range(count):
            start = step(index, start)
        return start
    return lax.fori_loop(0, count, step, start)


def place_in_axis():
    position = lax.axis_index("ctx")
    pair = position // 2
    return position, pair, position - 2 * pair


def rows_of(head, rows, base=0):
    return slice(base + head * rows, base + (head + 1) * rows)


def run_of(half):
    return next(run for run in (4, 2, 1) if half % run == 0)


def side_by_side(ref, slot, half, lines):
    return jnp.concatenate([ref[slot + step, lines, :] for step in range(run_of(half))], axis=1)


def later(ref, slot, half, lines):
    parts = []
    for step in range(run_of(half)):
        at = slot + step
        held = ref[jnp.minimum(at, half - 1), lines, :]
        parts.append(jnp.where(at < half, held, jnp.zeros_like(held)))
    return jnp.concatenate(parts, axis=1)


def times(left, right):
    return lax.dot_general(left, right, (((1,), (1,)), ((), ())), preferred_element_type=jnp.float32)


def own_kernel(heads, mine_ref, even_ref, shifted_ref):
    half, span, _ = mine_ref.shape
    rows = (span - EXTRA) // (2 * heads)
    base = heads * rows + EXTRA
    _, pair, core = place_in_axis()
    for head in range(heads):

        def step(index, total):
            slot = index * run_of(half)
            left = side_by_side(mine_ref, slot, half, rows_of(head, rows, base))
            return total + times(left, later(mine_ref, slot + pair + core, half, rows_of(head, rows, EXTRA)))

        even_ref[head] = repeat(half // run_of(half), step, jnp.zeros((rows, rows), jnp.float32))

    def shift(slot, carry):
        at = slot + pair + 1 - core
        held = mine_ref[jnp.minimum(at, half - 1), EXTRA : EXTRA + heads * rows, :]
        shifted_ref[slot] = jnp.where(at < half, held, jnp.zeros_like(held))
        return carry

    repeat(half, shift, 0)


def toeplitz_kernel(heads, mine_ref, lead_ref, toeplitz_ref, lags_ref):
    half, span, _ = mine_ref.shape
    rows = (span - EXTRA) // (2 * heads)
    blocks = 2 * half
    position, _, core = place_in_axis()
    lags_ref[:, : (blocks + 1) * rows] = jnp.zeros((EXTRA, (blocks + 1) * rows), jnp.float32)

    def place(slot, carry):
        for held, parity in ((mine_ref[slot, :EXTRA, :], core), (lead_ref[slot, :EXTRA, :], 1 - core)):
            at = pl.multiple_of((blocks + 1 + 2 * slot + parity) * rows, rows)
            lags_ref[:, pl.ds(at, rows)] = held.astype(jnp.float32)
        return carry

    repeat(half, place, 0)
    reach = (blocks + 1) * rows
    start = pl.multiple_of((blocks - position) * rows, rows)
    window = lags_ref[:, pl.ds(start, reach)]
    for head in range(heads):
        lines = jnp.broadcast_to(window[head : head + 1], (rows, reach)).astype(toeplitz_ref.dtype)
        skewed = pltpu.roll(lines, 0, 1, stride=1, stride_axis=0)
        toeplitz_ref[head] = skewed[:, rows:]


def input_sums(toeplitz_ref, mine_ref, ref, head, half, rows, core, others):
    lines = rows_of(head, rows, EXTRA)

    def gather(index, total):
        left, right = [], []
        for nth in range(run_of(half)):
            slot = index * run_of(half) + nth
            for at, block in ((2 * slot + core, mine_ref[slot, lines, :]), (2 * slot + 1 - core, ref[slot, others, :])):
                left.append(toeplitz_ref[head, :, pl.ds(pl.multiple_of(at * rows, rows), rows)])
                right.append(block)
        return total + jnp.dot(
            jnp.concatenate(left, axis=1), jnp.concatenate(right, axis=0), preferred_element_type=jnp.float32
        )

    return repeat(half // run_of(half), gather, jnp.zeros((rows, mine_ref.shape[2]), jnp.float32))


def input_kernel(heads, factor, mine_ref, lead_ref, toeplitz_ref, out_ref, odd_ref, shifted_ref):
    half, span, width = mine_ref.shape
    rows = (span - EXTRA) // (2 * heads)
    base = heads * rows + EXTRA
    lead = (lead_ref.shape[1] - EXTRA) // rows
    _, pair, core = place_in_axis()
    for head in range(lead):
        total = input_sums(toeplitz_ref, mine_ref, lead_ref, head, half, rows, core, rows_of(head, rows, EXTRA))
        out_ref[:, head * width : (head + 1) * width] = (total * factor).astype(out_ref.dtype)
    for head in range(lead):

        def step(index, total):
            slot = index * run_of(half)
            left = side_by_side(mine_ref, slot, half, rows_of(head, rows, base))
            right = later(lead_ref, slot + pair + core, half, rows_of(head, rows, EXTRA))
            for nth in range(run_of(half)):
                shifted_ref[slot + nth, rows_of(head, rows), :] = right[:, nth * width : (nth + 1) * width]
            return total + times(left, right)

        odd_ref[head] = repeat(half // run_of(half), step, jnp.zeros((rows, rows), jnp.float32))


def filter_kernel(
    heads,
    factor,
    mine_ref,
    rest_ref,
    own_ref,
    other_ref,
    toeplitz_ref,
    even_ref,
    odd_ref,
    held_ref,
    out_ref,
    terms_ref,
    out_vmem,
    terms_vmem,
    sems,
):
    half, span, width = mine_ref.shape
    rows = (span - EXTRA) // (2 * heads)
    base = heads * rows + EXTRA
    lead = other_ref.shape[1] // rows
    behind = (heads - lead) * rows
    _, pair, core = place_in_axis()
    output = pltpu.make_async_copy(held_ref, out_ref.at[:, pl.ds(0, lead * width)], sems.at[0])
    output.start()
    for head in range(lead, heads):
        total = input_sums(toeplitz_ref, mine_ref, rest_ref, head, half, rows, core, rows_of(head - lead, rows))
        out_vmem[:, (head - lead) * width : (head - lead + 1) * width] = (total * factor).astype(out_vmem.dtype)
    final = pltpu.make_async_copy(out_vmem, out_ref.at[:, pl.ds(lead * width, (heads - lead) * width)], sems.at[2])
    final.start()
    source = lax.broadcasted_iota(jnp.int32, (rows, rows), 0)
    target = lax.broadcasted_iota(jnp.int32, (rows, rows), 1)
    first = (target >= source) == (core == 0)
    sums = []
    for head in range(heads):
        lines = rows_of(head, rows)

        def step(index, totals):
            even, odd = totals
            slot = index * run_of(half)
            left = side_by_side(rest_ref, slot, half, rows_of(head, rows, behind))
            if head < lead:
                other = side_by_side(other_ref, slot, half, lines)
            else:
                other = later(rest_ref, slot + pair + core, half, rows_of(head - lead, rows))
                odd = odd + times(side_by_side(mine_ref, slot, half, rows_of(head, rows, base)), other)
            both = times(left, jnp.concatenate([other, side_by_side(own_ref, slot, half, lines)], axis=0))
            return even + both[:, :rows], odd + both[:, rows:]

        begin = odd_ref[head] if head < lead else jnp.zeros((rows, rows), jnp.float32)
        even, odd = repeat(half // run_of(half), step, (even_ref[head], begin))
        terms = jnp.where(first, even, odd)
        folded = terms[0:8]
        for group in range(1, rows // 8):
            folded = folded + pltpu.roll(terms[8 * group : 8 * group + 8], rows - 8 * group, 1)
        sums.append(folded)
    folded = jnp.concatenate(sums, axis=0)
    line = lax.broadcasted_iota(jnp.int32, folded.shape, 0) & 7
    terms = jnp.where(line == 0, folded, 0.0)
    for shift in range(1, 8):
        terms = terms + jnp.where(line == shift, pltpu.roll(folded, rows - shift, 1), 0.0)
    for head in range(heads):
        terms_vmem[head : head + 1, :] = jnp.sum(terms[8 * head : 8 * head + 8], axis=0, keepdims=True) * factor
    last = pltpu.make_async_copy(terms_vmem, terms_ref, sems.at[1])
    last.start()
    output.wait()
    final.wait()
    last.wait()


def call(kernel, args, out_shape, out_specs, scratch=(), scratch_bytes=0, in_specs=None, micros=1.0):
    return pl.pallas_call(
        kernel,
        out_shape=out_shape,
        in_specs=in_specs or [ON_CHIP] * len(args),
        out_specs=out_specs,
        scratch_shapes=list(scratch),
        compiler_params=pltpu.CompilerParams(vmem_limit_bytes=min(scratch_bytes + (4 << 20), 60 << 20)),
        cost_estimate=pl.CostEstimate(flops=int(micros * 1e9), bytes_accessed=int(micros * 3e6), transcendentals=0),
    )(*args)


def body(inputs, grad_out, filter_w):
    rows, channels = inputs.shape
    heads = filter_w.shape[0]
    blocks = lax.axis_size("ctx")
    half = blocks // 2
    factor = float(rows * blocks) ** (-0.5)
    kind = inputs.dtype
    width = channels // heads
    base = heads * rows + EXTRA
    span = base + heads * rows
    shape = jax.ShapeDtypeStruct
    swaps = [(index, index ^ 1) for index in range(blocks)]
    payload = call(
        pack_kernel,
        [pltpu.with_memory_space_constraint(each, pltpu.HBM) for each in (grad_out, inputs, filter_w)],
        shape((span, width), kind),
        ON_CHIP,
        [VMEM(filter_w.shape, filter_w.dtype), pltpu.SemaphoreType.DMA((1 + 2 * heads,))],
        in_specs=[pl.BlockSpec(memory_space=pltpu.HBM)] * 3,
    )
    groups = [[2 * slot + core for slot in range(half)] for core in range(2)]
    mine = lax.all_gather(payload, "ctx", axis=0, tiled=False, axis_index_groups=groups)
    ahead = heads - 1
    cut = EXTRA + ahead * rows
    lead = lax.ppermute(mine[:, :cut], "ctx", swaps)
    rest = lax.ppermute(mine[:, cut:], "ctx", swaps)
    square = shape((heads, rows, rows), jnp.float32)
    shifted = shape((half, heads * rows, width), kind)
    even, own = call(functools.partial(own_kernel, heads), [mine], (square, shifted), (ON_CHIP, ON_CHIP))
    toeplitz = call(
        functools.partial(toeplitz_kernel, heads),
        [mine, lead],
        shape((heads, rows, blocks * rows), kind),
        ON_CHIP,
        [VMEM((EXTRA, (2 * blocks + 1) * rows), jnp.float32)],
        4 * EXTRA * (2 * blocks + 1) * rows,
    )
    held, odd, other = call(
        functools.partial(input_kernel, heads, factor),
        [mine, lead, toeplitz],
        (
            shape((rows, ahead * width), kind),
            shape((ahead, rows, rows), jnp.float32),
            shape((half, ahead * rows, width), kind),
        ),
        (ON_CHIP, ON_CHIP, ON_CHIP),
    )
    return call(
        functools.partial(filter_kernel, heads, factor),
        [mine, rest, own, other, toeplitz, even, odd, held],
        (shape((rows, channels), kind), shape((heads, rows), jnp.float32)),
        (ANYWHERE, ANYWHERE),
        [VMEM((rows, channels - ahead * width), kind), VMEM((heads, rows), jnp.float32), pltpu.SemaphoreType.DMA((3,))],
    )


def solution(mesh):
    placed = (P("ctx", "ch"), P("ctx", "ch"), P("ch", "ctx"))
    return jax.shard_map(
        body,
        mesh=mesh,
        in_specs=placed,
        out_specs=(P("ctx", "ch"), P("ch", "ctx")),
        check_vma=False,
    )
```

```python
import functools

import jax
import jax.numpy as jnp
from jax import lax
from jax.experimental import pallas as pl
from jax.experimental.pallas import tpu as pltpu
from jax.sharding import PartitionSpec as P


EXTRA = 8
VMEM = pltpu.VMEM
ANYWHERE = pl.BlockSpec(memory_space=pl.ANY)
ON_CHIP = pl.BlockSpec(memory_space=VMEM)


def pack_kernel(grad_ref, input_ref, filter_ref, out_ref, filter_vmem, sems):
    rows = grad_ref.shape[0]
    heads, width = filter_ref.shape
    base = heads * rows + EXTRA
    copies = [pltpu.make_async_copy(filter_ref, filter_vmem, sems.at[0])]
    for head in range(heads):
        lanes = pl.ds(head * width, width)
        for ref, start, nth in ((grad_ref, 0, 1), (input_ref, base, 2)):
            into = out_ref.at[pl.ds(start + head * rows, rows)]
            copies.append(pltpu.make_async_copy(ref.at[:, lanes], into, sems.at[2 * head + nth]))
    for copy in copies[1:] + copies[:1]:
        copy.start()
    copies[0].wait()
    block = filter_vmem[...].astype(jnp.float32)
    block = jnp.concatenate([block, jnp.zeros((EXTRA - heads, width), jnp.float32)], axis=0)
    out_ref[heads * rows : base, :] = block.astype(out_ref.dtype)
    for copy in copies[1:]:
        copy.wait()


def repeat(count, step, start):
    if count <= 4:
        for index in range(count):
            start = step(index, start)
        return start
    return lax.fori_loop(0, count, step, start)


def place_in_axis():
    position = lax.axis_index("ctx")
    pair = position // 2
    return position, pair, position - 2 * pair


def rows_of(head, rows, base=0):
    return slice(base + head * rows, base + (head + 1) * rows)


def run_of(half):
    return next(run for run in (4, 2, 1) if half % run == 0)


def side_by_side(ref, slot, half, lines):
    return jnp.concatenate([ref[slot + step, lines, :] for step in range(run_of(half))], axis=1)


def later(ref, slot, half, lines):
    parts = []
    for step in range(run_of(half)):
        at = slot + step
        held = ref[jnp.minimum(at, half - 1), lines, :]
        parts.append(jnp.where(at < half, held, jnp.zeros_like(held)))
    return jnp.concatenate(parts, axis=1)


def times(left, right):
    return lax.dot_general(left, right, (((1,), (1,)), ((), ())), preferred_element_type=jnp.float32)


def own_kernel(heads, mine_ref, even_ref, shifted_ref):
    half, span, _ = mine_ref.shape
    rows = (span - EXTRA) // (2 * heads)
    base = heads * rows + EXTRA
    _, pair, core = place_in_axis()
    for head in range(heads):

        def step(index, total):
            slot = index * run_of(half)
            left = side_by_side(mine_ref, slot, half, rows_of(head, rows, base))
            return total + times(left, later(mine_ref, slot + pair + core, half, rows_of(head, rows)))

        even_ref[head] = repeat(half // run_of(half), step, jnp.zeros((rows, rows), jnp.float32))

    def shift(slot, carry):
        at = slot + pair + 1 - core
        held = mine_ref[jnp.minimum(at, half - 1), : heads * rows, :]
        shifted_ref[slot] = jnp.where(at < half, held, jnp.zeros_like(held))
        return carry

    repeat(half, shift, 0)


def toeplitz_kernel(heads, mine_ref, filter_ref, toeplitz_ref, lags_ref):
    half, span, _ = mine_ref.shape
    rows = (span - EXTRA) // (2 * heads)
    blocks = 2 * half
    position, _, core = place_in_axis()
    lags_ref[:, : (blocks + 1) * rows] = jnp.zeros((EXTRA, (blocks + 1) * rows), jnp.float32)

    def place(slot, carry):
        for held, parity in ((mine_ref[slot, heads * rows : heads * rows + EXTRA, :], core), (filter_ref[slot], 1 - core)):
            at = pl.multiple_of((blocks + 1 + 2 * slot + parity) * rows, rows)
            lags_ref[:, pl.ds(at, rows)] = held.astype(jnp.float32)
        return carry

    repeat(half, place, 0)
    reach = (blocks + 1) * rows
    start = pl.multiple_of((blocks - position) * rows, rows)
    window = lags_ref[:, pl.ds(start, reach)]
    for head in range(heads):
        lines = jnp.broadcast_to(window[head : head + 1], (rows, reach)).astype(toeplitz_ref.dtype)
        skewed = pltpu.roll(lines, 0, 1, stride=1, stride_axis=0)
        toeplitz_ref[head] = skewed[:, rows:]


def input_kernel(heads, factor, mine_ref, grad_ref, toeplitz_ref, out_ref, odd_ref, shifted_ref):
    half, span, width = mine_ref.shape
    rows = (span - EXTRA) // (2 * heads)
    base = heads * rows + EXTRA
    _, pair, core = place_in_axis()
    for head in range(heads):
        lines = rows_of(head, rows)

        def gather(slot, total):
            own = pl.multiple_of((2 * slot + core) * rows, rows)
            other = pl.multiple_of((2 * slot + 1 - core) * rows, rows)
            left = jnp.concatenate(
                [toeplitz_ref[head, :, pl.ds(own, rows)], toeplitz_ref[head, :, pl.ds(other, rows)]], axis=1
            )
            both = jnp.concatenate([mine_ref[slot, lines, :], grad_ref[slot, lines, :]], axis=0)
            return total + jnp.dot(left, both, preferred_element_type=jnp.float32)

        total = repeat(half, gather, jnp.zeros((rows, width), jnp.float32))
        out_ref[:, head * width : (head + 1) * width] = (total * factor).astype(out_ref.dtype)
    for head in range(heads):

        def step(index, total):
            slot = index * run_of(half)
            left = side_by_side(mine_ref, slot, half, rows_of(head, rows, base))
            right = later(grad_ref, slot + pair + core, half, rows_of(head, rows))
            for nth in range(run_of(half)):
                shifted_ref[slot + nth, rows_of(head, rows), :] = right[:, nth * width : (nth + 1) * width]
            return total + times(left, right)

        odd_ref[head] = repeat(half // run_of(half), step, jnp.zeros((rows, rows), jnp.float32))


def filter_kernel(
    heads, factor, own_ref, other_ref, input_ref, even_ref, odd_ref, held_ref, out_ref, terms_ref, terms_vmem, sems
):
    half, lines, _ = input_ref.shape
    rows = lines // heads
    _, _, core = place_in_axis()
    output = pltpu.make_async_copy(held_ref, out_ref, sems.at[0])
    output.start()
    source = lax.broadcasted_iota(jnp.int32, (rows, rows), 0)
    target = lax.broadcasted_iota(jnp.int32, (rows, rows), 1)
    first = (target >= source) == (core == 0)
    sums = []
    for head in range(heads):
        lines = rows_of(head, rows)

        def step(index, total):
            slot = index * run_of(half)
            left = side_by_side(input_ref, slot, half, lines)
            right = jnp.concatenate(
                [side_by_side(other_ref, slot, half, lines), side_by_side(own_ref, slot, half, lines)], axis=0
            )
            return total + times(left, right)

        products = repeat(half // run_of(half), step, jnp.zeros((rows, 2 * rows), jnp.float32))
        even = products[:, :rows] + even_ref[head]
        odd = products[:, rows:] + odd_ref[head]
        terms = jnp.where(first, even, odd)
        folded = terms[0:8]
        for group in range(1, rows // 8):
            folded = folded + pltpu.roll(terms[8 * group : 8 * group + 8], rows - 8 * group, 1)
        sums.append(folded)
    folded = jnp.concatenate(sums, axis=0)
    line = lax.broadcasted_iota(jnp.int32, folded.shape, 0) & 7
    terms = jnp.where(line == 0, folded, 0.0)
    for shift in range(1, 8):
        terms = terms + jnp.where(line == shift, pltpu.roll(folded, rows - shift, 1), 0.0)
    for head in range(heads):
        terms_vmem[head : head + 1, :] = jnp.sum(terms[8 * head : 8 * head + 8], axis=0, keepdims=True) * factor
    last = pltpu.make_async_copy(terms_vmem, terms_ref, sems.at[1])
    last.start()
    output.wait()
    last.wait()


def call(kernel, args, out_shape, out_specs, scratch=(), scratch_bytes=0, in_specs=None, micros=1.0):
    return pl.pallas_call(
        kernel,
        out_shape=out_shape,
        in_specs=in_specs or [ON_CHIP] * len(args),
        out_specs=out_specs,
        scratch_shapes=list(scratch),
        compiler_params=pltpu.CompilerParams(vmem_limit_bytes=min(scratch_bytes + (4 << 20), 60 << 20)),
        cost_estimate=pl.CostEstimate(flops=int(micros * 1e9), bytes_accessed=int(micros * 3e6), transcendentals=0),
    )(*args)


def body(inputs, grad_out, filter_w):
    rows, channels = inputs.shape
    heads = filter_w.shape[0]
    blocks = lax.axis_size("ctx")
    half = blocks // 2
    factor = float(rows * blocks) ** (-0.5)
    kind = inputs.dtype
    width = channels // heads
    base = heads * rows + EXTRA
    span = base + heads * rows
    shape = jax.ShapeDtypeStruct
    swaps = [(index, index ^ 1) for index in range(blocks)]
    payload = call(
        pack_kernel,
        [pltpu.with_memory_space_constraint(each, pltpu.HBM) for each in (grad_out, inputs, filter_w)],
        shape((span, width), kind),
        ON_CHIP,
        [VMEM(filter_w.shape, filter_w.dtype), pltpu.SemaphoreType.DMA((1 + 2 * heads,))],
        in_specs=[pl.BlockSpec(memory_space=pltpu.HBM)] * 3,
    )
    groups = [[2 * slot + core for slot in range(half)] for core in range(2)]
    mine = lax.all_gather(payload, "ctx", axis=0, tiled=False, axis_index_groups=groups)
    filters = lax.ppermute(mine[:, heads * rows : base], "ctx", swaps)
    grads = lax.ppermute(mine[:, : heads * rows], "ctx", swaps)
    others = lax.ppermute(mine[:, base:], "ctx", swaps)
    square = shape((heads, rows, rows), jnp.float32)
    shifted = shape((half, heads * rows, width), kind)
    even, own = call(functools.partial(own_kernel, heads), [mine], (square, shifted), (ON_CHIP, ON_CHIP))
    toeplitz = call(
        functools.partial(toeplitz_kernel, heads),
        [mine, filters],
        shape((heads, rows, blocks * rows), kind),
        ON_CHIP,
        [VMEM((EXTRA, (2 * blocks + 1) * rows), jnp.float32)],
        4 * EXTRA * (2 * blocks + 1) * rows,
    )
    held, odd, other = call(
        functools.partial(input_kernel, heads, factor),
        [mine, grads, toeplitz],
        (shape((rows, channels), kind), square, shifted),
        (ON_CHIP, ON_CHIP, ON_CHIP),
    )
    return call(
        functools.partial(filter_kernel, heads, factor),
        [own, other, others, even, odd, held],
        (shape((rows, channels), kind), shape((heads, rows), jnp.float32)),
        (ANYWHERE, ANYWHERE),
        [VMEM((heads, rows), jnp.float32), pltpu.SemaphoreType.DMA((2,))],
    )


def solution(mesh):
    placed = (P("ctx", "ch"), P("ctx", "ch"), P("ch", "ctx"))
    return jax.shard_map(
        body,
        mesh=mesh,
        in_specs=placed,
        out_specs=(P("ctx", "ch"), P("ch", "ctx")),
        check_vma=False,
    )
```
